256 devices in a mesh: band: 32 (over z, y_lo, core), pw: 8 (over y_hi, x).
Axes of the slice: x: 4, y: 4 (y_hi: 2, y_lo: 2; y = y_hi * 2 + y_lo), z: 8, core: 2. Of those that a mesh axis runs over, the one named last changes fastest.
Arguments:
- elements: bfloat16 [64, 4096, 256], P('band', 'pw'), may hold values from -8 to 8
- strength: bfloat16 [4096, 4096], P('pw', 'band'), may hold values from -6 to 6
- pole_freq: bfloat16 [4096, 4096], P('pw', 'band'), may hold values from 0.5 to 4
- energies: float32 [64], P('band'), may hold values from -2 to 2
- imag_freqs: float32 [2], replicated, may hold values from 0.25 to 2
Outputs:
- sigma: float32 [2, 256, 256], P(None, 'band', 'pw')
The draws below stay inside these ranges and needn't reach their ends.
All inputs are finite; a program needn't handle non-finite values.
Results may differ from the reference program's by a relative error of at most 0.006.
Values may be sent and summed in bfloat16 or wider, within the bound.
No kernel may reach another device: no remote copies, remote signals or barrier semaphores. Data moves between devices by JAX's collectives and lax.ppermute only.
A program may use at most 64 MiB of HBM per device.

```python
import math
import jax
import jax.numpy as jnp
from jax import lax

NS = 256
BAND_DEV = 2
NG = 4096
HB = 256
NBANDS = 64


def draw_elements(key, part):
    first, second = jax.random.split(jax.random.fold_in(key, 11), 2)
    shape = (NBANDS, NG, NS)
    base = jax.random.normal(first, shape, jnp.float32)
    groups = NBANDS // BAND_DEV
    pairing = jax.random.permutation(second, groups)
    band_group = jnp.arange(NBANDS) // BAND_DEV
    state_group = jnp.arange(NS) // (NS // groups)
    hit = pairing[band_group][:, None] == state_group[None, :]
    factor = jnp.where(hit, 2.5, 1.0)[:, None, :]
    return jnp.clip(base * factor, -8.0, 8.0).astype(jnp.bfloat16)


def draw_strength(key, part):
    first = jax.random.fold_in(jax.random.fold_in(key, 23), 0)
    shape = (NG, NG)
    base = jax.random.normal(first, shape, jnp.float32)
    return jnp.clip(base, -6.0, 6.0).astype(jnp.bfloat16)


def block_scale(stream_key, dims, cuts, least, largest):
    def one(dim, shards_of):
        heights = jax.random.uniform(jax.random.fold_in(jax.random.fold_in(stream_key, 6), dim), (shards_of,), jnp.float32, least / len(cuts), largest / len(cuts))
        return jnp.repeat(jnp.exp(heights), dims[dim] // shards_of).reshape((-1,) + (1,) * (len(dims) - dim - 1))

    gain = one(*cuts[0])
    for cut in cuts[1:]:
        gain = gain * one(*cut)
    return gain


def setup_inputs(seed: int = 0) -> dict:
    arg_keys = jax.random.split(jax.random.key(seed), 6)
    return {
        "elements": draw_elements(jax.random.fold_in(arg_keys[5], 71), 0),
        "strength": draw_strength(jax.random.fold_in(arg_keys[5], 71), 0),
        "pole_freq": jnp.clip(jnp.exp(math.log(4.0) - 2.0794415 * jax.random.uniform(arg_keys[2], (NG, NG), jnp.float32) ** block_scale(arg_keys[2], (NG, NG), ((0, 8), (1, 32)), -0.2, 0.2)), 0.5, 4.0).astype(jnp.bfloat16),
        "energies": jnp.clip(jax.random.uniform(arg_keys[3], (NBANDS,), jnp.float32, -2.0, 2.0) * block_scale(arg_keys[3], (NBANDS,), ((0, 32),), -0.4, 0.0), -2.0, 2.0),
        "imag_freqs": jnp.clip(jnp.exp(jax.random.uniform(arg_keys[4], (2,), jnp.float32, math.log(0.25), math.log(2.0))), 0.25, 2.0),
    }


def reference(elements, strength, pole_freq, energies, imag_freqs):
    nu_square = imag_freqs * imag_freqs
    strength_f = strength.astype(jnp.float32)
    pole_f = pole_freq.astype(jnp.float32)

    def one_band(running, inputs):
        band_rows, energy = inputs
        shifted = pole_f + energy
        kernel = (strength_f[None] * shifted[None] / (nu_square[:, None, None] + shifted[None] * shifted[None])).astype(jnp.bfloat16)
        rows_f = band_rows.astype(jnp.float32).reshape(NG // HB, HB, NS)
        kern_f = kernel.astype(jnp.float32).reshape(2, NG // HB, HB, NG)
        partial_value = jnp.einsum('rgn,ergc->ernc', rows_f, kern_f, precision=lax.Precision.HIGHEST).astype(jnp.bfloat16)
        running = running + jnp.einsum('ernc,cm->enm', partial_value.astype(jnp.float32), band_rows.astype(jnp.float32), precision=lax.Precision.HIGHEST)
        return (running, None)
    start = jnp.zeros((2, NS, NS), jnp.float32)
    total = lax.scan(one_band, start, (elements, energies))[0]
    return total / (NG * math.sqrt(NBANDS))
```

```python
import functools
import math

import jax
import jax.numpy as jnp
from jax import lax
from jax.experimental import pallas as pl
from jax.experimental.pallas import tpu as pltpu
from jax.sharding import Mesh
from jax.sharding import PartitionSpec as P

INTERPRET = False

SIZES = {"z": 8, "yl": 2, "c": 2, "yh": 2, "x": 4}
BAND = ("z", "yl", "c")
PW = ("yh", "x")
F32 = jnp.float32
BF16 = jnp.bfloat16


def move(value, axes, target):
    sizes = [SIZES[axis] for axis in axes]
    total = math.prod(sizes)

    def flat(indices):
        out = 0
        for index, size in zip(indices, sizes):
            out = out * size + index % size
        return out

    pairs = []
    for source in range(total):
        rest, indices = source, []
        for size in reversed(sizes):
            indices.append(rest % size)
            rest //= size
        pairs.append((source, flat(target(*reversed(indices)))))
    return lax.ppermute(value, axes, pairs)


def sum_kernel(count, first, last, scale, *refs):
    where, energies, nu = refs[:3]
    pieces = refs[3 : 3 + count]
    rows = refs[3 + count : 7 + count]
    columns = refs[7 + count : 15 + count]
    rest = refs[15 + count :]
    if first:
        out, scr, cols = rest[0], rest[1], rest[2]
        total = out
    else:
        before, out, scr, cols, total = rest
    nu0 = nu[0] * nu[0]
    nu1 = nu[1] * nu[1]
    width = pieces[0].shape[2]
    states = rows[0].shape[2]

    for slot in range(count):
        for part in range(2):
            scr[slot, part] = pieces[slot][part].astype(F32).T
    for dx in range(4):
        for core in range(2):
            cols[dx, core] = columns[2 * dx + core][...]
    if first:
        total[...] = jnp.zeros_like(total)
    else:
        total[...] = before[...]

    def one_piece(slot, carry):
        dx = where[2 * slot]
        flip = where[2 * slot + 1]
        strength = scr[slot, 0]
        pole = scr[slot, 1]
        for pair in range(4):
            part0, part1 = [], []
            for k in range(2):
                shifted = pole + energies[2 * pair + k]
                square = shifted * shifted
                low = square + nu0
                high = square + nu1
                common = strength * shifted * pl.reciprocal(low * high)
                kern0 = (common * high).astype(BF16)
                kern1 = (common * low).astype(BF16)
                both = jnp.concatenate([kern0, kern1], axis=0)
                value = jnp.dot(both, rows[pair][k], preferred_element_type=F32).astype(BF16)
                part0.append(value[:width])
                part1.append(value[width:])
            left = cols[dx, where[16 + pair], 2 * where[20 + pair] + flip]
            total[0] += jnp.dot(left, jnp.concatenate(part0, axis=0), preferred_element_type=F32)
            total[1] += jnp.dot(left, jnp.concatenate(part1, axis=0), preferred_element_type=F32)
        return carry

    lax.fori_loop(0, count, one_piece, 0)
    if not first:
        blocks, tall = out.shape[0], out.shape[1] // 2
        for block in range(blocks):
            for e in range(2):
                out[block, pl.ds(e * tall, tall), :] = (
                    total[e, pl.ds(block * tall, tall), :] * scale
                ).astype(BF16)


def run_sum(first, scale, where, energies, nu, pieces, rows, columns, before=None):
    count = len(pieces)
    group, height, width = pieces[0].shape
    states = rows[0].shape[2]
    smem = pl.BlockSpec(memory_space=pltpu.SMEM)
    vmem = pl.BlockSpec(memory_space=pltpu.VMEM)
    operands = [where, energies, nu, *pieces, *rows, *columns]
    specs = [smem] * 3 + [vmem] * (len(operands) - 3)
    scratch = [
        pltpu.VMEM((count, 2, width, height), F32),
        pltpu.VMEM((4, 2) + columns[0].shape, BF16),
    ]
    if first:
        out_shape = jax.ShapeDtypeStruct((2, states, states), F32)
    else:
        operands.append(before)
        specs.append(vmem)
        scratch.append(pltpu.VMEM((2, states, states), F32))
        out_shape = jax.ShapeDtypeStruct((8, states // 4, states), BF16)
    flops = count * 8 * 2 * 2 * (width * height * states + width * states * states)
    return pl.pallas_call(
        functools.partial(sum_kernel, count, first, not first, scale),
        out_shape=out_shape,
        in_specs=specs,
        out_specs=vmem,
        scratch_shapes=scratch,
        compiler_params=pltpu.CompilerParams(vmem_limit_bytes=32 * 1024 * 1024),
        cost_estimate=pl.CostEstimate(
            flops=flops, bytes_accessed=8 * 1024 * 1024, transcendentals=count * 8 * width * height
        ),
        interpret=INTERPRET,
        name="first_sum" if first else "last_sum",
    )(*operands)


def turn_kernel(states, piece, mine, other0, other1, other2, out):
    width = other0.shape[1]
    start = pl.multiple_of(piece[0], width)
    own = mine[:, pl.ds(start, width), :]
    for slot, value in enumerate((own, other0[...], other1[...], other2[...])):
        out[slot] = value.reshape(2 * width, states).T


def turn(piece, mine, others):
    width, states = others[0].shape[1:]
    smem = pl.BlockSpec(memory_space=pltpu.SMEM)
    vmem = pl.BlockSpec(memory_space=pltpu.VMEM)
    return pl.pallas_call(
        functools.partial(turn_kernel, states),
        out_shape=jax.ShapeDtypeStruct((4, states, 2 * width), BF16),
        in_specs=[smem] + [vmem] * 4,
        out_specs=vmem,
        compiler_params=pltpu.CompilerParams(vmem_limit_bytes=8 * 1024 * 1024),
        interpret=INTERPRET,
        name="turn",
    )(piece, mine, *others)


def half_kernel(got, out):
    out[...] = jnp.sum(got[...].astype(F32), axis=0).T.astype(BF16)


def end_kernel(got, out):
    out[...] = jnp.sum(got[...].astype(F32), axis=0)


def small(body, value, out_shape, name):
    vmem = pl.BlockSpec(memory_space=pltpu.VMEM)
    return pl.pallas_call(
        body,
        out_shape=out_shape,
        in_specs=[vmem],
        out_specs=vmem,
        compiler_params=pltpu.CompilerParams(vmem_limit_bytes=8 * 1024 * 1024),
        interpret=INTERPRET,
        name=name,
    )(value)


def on_device(elements, strength, pole_freq, energies, imag_freqs):
    band_count, row_count, states = elements.shape
    width = strength.shape[1]
    z = lax.axis_index("z")
    yl = lax.axis_index("yl")
    c = lax.axis_index("c")
    yh = lax.axis_index("yh")
    x = lax.axis_index("x")
    total_rows = row_count * 8
    scale = 1.0 / (total_rows * math.sqrt(band_count * 32))

    own = jnp.stack((strength, pole_freq))
    held = move(own, ("c", "yh"), lambda cc, hh: (hh, cc))

    def piece_for(a, b):
        start = ((yl ^ a) * 2 + (yh ^ b)) * width
        value = lax.dynamic_slice_in_dim(elements, start, width, 1)
        return move(value, ("yl", "yh"), lambda l, h: (l ^ a, h ^ b))

    others = [piece_for(0, 1), piece_for(1, 0), piece_for(1, 1)]

    rows, levels = [], []
    for a in range(2):
        for b in range(2):
            target = functools.partial(lambda a, b, l, cc, h: (l ^ a, h, cc ^ b), a, b)
            rows.append(move(elements, ("yl", "c", "yh"), target))
            levels.append(move(energies, ("yl", "c", "yh"), target))
    levels = jnp.concatenate(levels)

    up, down = held, held
    pieces = {0: held}
    for step in range(1, 4):
        up = move(up, ("z",), lambda i: (i + 1,))
        down = move(down, ("z",), lambda i: (i - 1,))
        pieces[-step], pieces[step] = up, down
    last_up = move(up[0], ("z",), lambda i: (i + 1,))
    last_down = move(down[1], ("z",), lambda i: (i - 1,))
    pieces[4] = jnp.stack((last_up, last_down))

    turned = turn((yl * 2 + yh)[None] * width, elements, others)
    by_x = [
        turned,
        move(turned, ("x",), lambda i: (i - 1,)),
        move(turned, ("x",), lambda i: (i + 2,)),
        move(turned, ("x",), lambda i: (i + 1,)),
    ]
    columns = []
    for value in by_x:
        columns.append(value)
        columns.append(move(value, ("c",), lambda i: (i ^ 1,)))

    def where(slots):
        out = []
        for slot in slots:
            block = (z + slot) % 8
            out += [(block % 4 - x) % 4, (block // 4) ^ yh]
        out += [jnp.int32(0)] * (16 - len(out))
        out += [yh ^ b ^ c for a in range(2) for b in range(2)]
        out += [jnp.int32(a) for a in range(2) for b in range(2)]
        return jnp.stack(out).astype(jnp.int32)

    early, late = (0, -1, 1, -2, 2), (-3, 3, 4)
    running = run_sum(
        True, scale, where(early), levels, imag_freqs, [pieces[s] for s in early], rows, columns
    )
    blocks = run_sum(
        False, scale, where(late), levels, imag_freqs, [pieces[s] for s in late], rows, columns, running
    )
    got = lax.all_to_all(blocks, PW, 0, 0, tiled=True)
    part = small(half_kernel, got, jax.ShapeDtypeStruct((states, states // 4), BF16), "half")
    part = lax.all_to_all(part.reshape(32, states // 32, states // 4), BAND, 0, 0, tiled=True)
    done = small(end_kernel, part, jax.ShapeDtypeStruct((states // 32, states // 4), F32), "end")
    return done.reshape(states // 32, 2, states // 8).transpose(1, 0, 2)


def solution(mesh):
    fine = Mesh(mesh.devices.reshape(8, 2, 2, 2, 4), ("z", "yl", "c", "yh", "x"))
    in_specs = (P(BAND, PW, None), P(PW, BAND), P(PW, BAND), P(BAND), P())
    out_specs = P(None, BAND, PW)
    return jax.shard_map(
        on_device, mesh=fine, in_specs=in_specs, out_specs=out_specs, check_vma=False
    )
```

```python
import functools
import math

import jax
import jax.numpy as jnp
from jax import lax
from jax.experimental import pallas as pl
from jax.experimental.pallas import tpu as pltpu
from jax.sharding import Mesh
from jax.sharding import PartitionSpec as P


INTERPRET = False
FRONT_VMEM = 64 * 1024 * 1024 - 1600 * 1024

SIZES = {"z": 8, "yl": 2, "c": 2, "yh": 2, "x": 4}
BAND = ("z", "yl", "c")
PW = ("yh", "x")
F32 = jnp.float32
BF16 = jnp.bfloat16


def move(value, axes, target):
    sizes = [SIZES[axis] for axis in axes]
    total = math.prod(sizes)

    def flat(indices):
        out = 0
        for index, size in zip(indices, sizes):
            out = out * size + index % size
        return out

    pairs = []
    for source in range(total):
        rest, indices = source, []
        for size in reversed(sizes):
            indices.append(rest % size)
            rest //= size
        pairs.append((source, flat(target(*reversed(indices)))))
    return lax.ppermute(value, axes, pairs)


def load(copies, screen, wide):
    for copy in copies:
        copy.wait()
    for slot in range(wide.shape[0]):
        wide[slot] = screen[slot].astype(F32)


def fill(kern, wide, levels, nu, unit):
    slot, pair = unit // 4, unit % 4
    width = wide.shape[2]
    tile = min(16, width)
    for start in range(0, width, tile):
        here = pl.ds(start, tile)
        strength = wide[slot, 0, here, :]
        pole = wide[slot, 1, here, :]
        for k in range(2):
            shifted = pole + levels[2 * pair + k]
            square = shifted * shifted
            above = strength * shifted
            for e in range(2):
                below = square + nu[e] * nu[e]
                kern[k, pl.ds(e * width + start, tile), :] = (
                    above * pl.reciprocal(below)
                ).astype(BF16)


def rows_dot(kern, held, part, unit):
    pair = unit % 4
    width, height = kern.shape[1] // 2, kern.shape[2]
    for k in range(2):
        value = jnp.dot(
            kern[k], held[2 * pair + k, pl.ds(0, height), :], preferred_element_type=F32
        ).astype(BF16)
        part[0, pl.ds(k * width, width), :] = value[:width]
        part[1, pl.ds(k * width, width), :] = value[width:]


def read_levels(held, levels, height):
    for band in range(8):
        parts = held[band, pl.ds(height, 16), :].astype(F32)
        levels[band] = (parts[0:1] + parts[1:2] + parts[2:3])[0, 0]


def early_kernel(count, *refs):
    nu, pieces, rows = refs[0], refs[1 : 1 + count], refs[1 + count : 5 + count]
    parts, held, screen, wide, kern_a, kern_b, levels, sems = refs[5 + count :]
    height = wide.shape[3]
    copies = [
        pltpu.make_async_copy(pieces[slot], screen.at[slot], sems.at[slot]) for slot in range(count)
    ]
    for copy in copies:
        copy.start()
    for pair in range(4):
        for k in range(2):
            held[2 * pair + k] = rows[pair][k]
    read_levels(held, levels, height)
    load(copies, screen, wide)
    last = 4 * count - 1
    fill(kern_a, wide, levels, nu, 0)

    def four(step, carry):
        for unit in (4 * step, 4 * step + 2):
            fill(kern_b, wide, levels, nu, unit + 1)
            rows_dot(kern_a, held, parts.at[unit], unit)
            fill(kern_a, wide, levels, nu, jnp.minimum(unit + 2, last))
            rows_dot(kern_b, held, parts.at[unit + 1], unit + 1)
        return carry

    lax.fori_loop(0, count, four, 0)
    for unit in range(4 * count, parts.shape[0]):
        parts[unit] = jnp.zeros_like(parts[unit])


def late_kernel(count, scale, *refs):
    where, nu, held, early = refs[:4]
    flat = refs[4 : 5 + count]
    columns = refs[5 + count : 13 + count]
    out, screen, wide, cols, kern_a, kern_b, part_a, part_b, total, levels, sems = refs[13 + count :]
    height = wide.shape[3]
    copies = [
        pltpu.make_async_copy(flat[slot], screen.at[slot], sems.at[slot])
        for slot in range(count - 1)
    ]
    for part in range(2):
        copies.append(
            pltpu.make_async_copy(
                flat[count - 1 + part], screen.at[count - 1, part], sems.at[count - 1 + part]
            )
        )
    for copy in copies:
        copy.start()
    for dx in range(4):
        for core in range(2):
            cols[dx, core] = columns[2 * dx + core][...]
    total[...] = jnp.zeros_like(total)
    part_b[...] = jnp.zeros_like(part_b)
    read_levels(held, levels, height)
    load(copies, screen, wide)
    last = 4 * count - 1

    def columns_dot(part, slot, unit):
        pair = unit % 4
        left = cols[where[2 * slot], where[18 + pair], pair // 2 * 2 + where[2 * slot + 1]]
        total[0] += jnp.dot(left, part[0], preferred_element_type=F32)
        total[1] += jnp.dot(left, part[1], preferred_element_type=F32)

    fill(kern_a, wide, levels, nu, 0)

    def early_dots(unit):
        for other in (2 * unit, 2 * unit + 1):
            columns_dot(early.at[other], other // 4, other)

    def four(step, carry):
        for unit in (4 * step, 4 * step + 2):
            before = jnp.maximum(unit - 1, 0)
            fill(kern_b, wide, levels, nu, unit + 1)
            rows_dot(kern_a, held, part_a, unit)
            early_dots(unit)
            columns_dot(part_b, 6 + before // 4, before)
            fill(kern_a, wide, levels, nu, jnp.minimum(unit + 2, last))
            rows_dot(kern_b, held, part_b, unit + 1)
            early_dots(unit + 1)
            columns_dot(part_a, 6 + unit // 4, unit)
        return carry

    lax.fori_loop(0, count, four, 0)
    columns_dot(part_b, 6 + last // 4, last)
    blocks, tall = out.shape[0], out.shape[1] // 2
    for block in range(blocks):
        for e in range(2):
            out[block, pl.ds(e * tall, tall), :] = (
                total[e, pl.ds(block * tall, tall), :] * scale
            ).astype(BF16)


SMEM = pl.BlockSpec(memory_space=pltpu.SMEM)
VMEM = pl.BlockSpec(memory_space=pltpu.VMEM)
ANY = pl.BlockSpec(memory_space=pl.ANY)


def screen_scratch(count, width, height):
    return [
        pltpu.VMEM((count, 2, width, height), BF16),
        pltpu.VMEM((count, 2, width, height), F32),
    ]


def early_sum(nu, pieces, rows):
    count = len(pieces)
    _, width, height = pieces[0].shape
    states = rows[0].shape[2]
    kern = pltpu.VMEM((2, 2 * width, height), BF16)
    flops = count * 8 * 2 * 2 * width * height * states
    return pl.pallas_call(
        functools.partial(early_kernel, count),
        out_shape=(
            jax.ShapeDtypeStruct((24, 2, 2 * width, states), BF16),
            jax.ShapeDtypeStruct((8, height + 16, states), BF16),
        ),
        in_specs=[SMEM] + [ANY] * count + [VMEM] * 4,
        out_specs=(VMEM, VMEM),
        scratch_shapes=screen_scratch(count, width, height)
        + [kern, kern, pltpu.SMEM((8,), F32), pltpu.SemaphoreType.DMA((count,))],
        compiler_params=pltpu.CompilerParams(vmem_limit_bytes=16 * 1024 * 1024),
        cost_estimate=pl.CostEstimate(
            flops=flops,
            bytes_accessed=8 * 1024 * 1024,
            transcendentals=count * 16 * width * height,
        ),
        interpret=INTERPRET,
        name="early_sum",
    )(nu, *pieces, *rows)


def late_sum(scale, where, nu, held, early, flat, columns):
    count = len(flat) - 1
    width, height = flat[-1].shape
    states = held.shape[2]
    kern = pltpu.VMEM((2, 2 * width, height), BF16)
    part = pltpu.VMEM((2, 2 * width, states), BF16)
    flops = count * 8 * 2 * 2 * (width * height * states + 3 * width * states * states)
    return pl.pallas_call(
        functools.partial(late_kernel, count, scale),
        out_shape=jax.ShapeDtypeStruct((8, states // 4, states), BF16),
        in_specs=[SMEM] * 2 + [VMEM] * 2 + [ANY] * (count + 1) + [VMEM] * 8,
        out_specs=VMEM,
        scratch_shapes=screen_scratch(count, width, height)
        + [pltpu.VMEM((4, 2) + columns[0].shape, BF16), kern, kern, part, part]
        + [pltpu.VMEM((2, states, states), F32), pltpu.SMEM((8,), F32)]
        + [pltpu.SemaphoreType.DMA((count + 1,))],
        compiler_params=pltpu.CompilerParams(vmem_limit_bytes=20 * 1024 * 1024),
        cost_estimate=pl.CostEstimate(
            flops=flops,
            bytes_accessed=8 * 1024 * 1024,
            transcendentals=count * 16 * width * height,
        ),
        interpret=INTERPRET,
        name="late_sum",
    )(where, nu, held, early, *flat, *columns)


def front_kernel(starts, where, energies, strength, pole, elements, *refs):
    screen, own, part01, part10, part11, tall, loaded, sems = refs
    height, width = strength.shape
    copies = [
        pltpu.make_async_copy(strength, loaded.at[0], sems.at[0]),
        pltpu.make_async_copy(pole, loaded.at[1], sems.at[1]),
        pltpu.make_async_copy(elements, tall.at[:, pl.ds(0, height), :], sems.at[2]),
    ]
    for copy in copies:
        copy.start()
    shape = (16, tall.shape[2])
    line = lax.broadcasted_iota(jnp.int32, shape, 0)
    for k in range(2):
        level = jnp.full(shape, energies[k], F32)
        high = level.astype(BF16).astype(F32)
        middle = (level - high).astype(BF16).astype(F32)
        low = level - high - middle
        value = jnp.where(line == 0, high, jnp.where(line == 1, middle, low))
        tall[k, pl.ds(height, 16), :] = value.astype(BF16)
    copies[0].wait()
    copies[1].wait()
    for part in range(2):
        screen[part] = loaded[part].T
    copies[2].wait()
    for slot, out in enumerate((own, part01, part10, part11)):
        out[...] = tall[:, pl.ds(pl.multiple_of(starts[slot], width), width), :]


def front(starts, where, energies, strength, pole, elements):
    height, width = strength.shape
    states = elements.shape[2]
    smem = pl.BlockSpec(memory_space=pltpu.SMEM)
    vmem = pl.BlockSpec(memory_space=pltpu.VMEM)
    anywhere = pl.BlockSpec(memory_space=pltpu.HBM)
    piece = jax.ShapeDtypeStruct((2, width, states), BF16)
    return pl.pallas_call(
        front_kernel,
        out_shape=(
            jax.ShapeDtypeStruct((2, width, height), BF16),
            piece,
            piece,
            piece,
            piece,
            jax.ShapeDtypeStruct((2, height + 16, states), BF16),
        ),
        in_specs=[smem] * 3 + [anywhere] * 3,
        out_specs=(vmem,) * 6,
        scratch_shapes=[pltpu.VMEM((2, height, width), BF16), pltpu.SemaphoreType.DMA((3,))],
        compiler_params=pltpu.CompilerParams(vmem_limit_bytes=FRONT_VMEM),
        interpret=INTERPRET,
        name="front",
    )(starts, where, energies, strength, pole, elements)


def turn_kernel(own, other0, other1, other2, out):
    width, states = own.shape[1:]
    for slot, ref in enumerate((own, other0, other1, other2)):
        out[slot] = ref[...].reshape(2 * width, states).T


def turn(own, others):
    width, states = own.shape[1:]
    vmem = pl.BlockSpec(memory_space=pltpu.VMEM)
    return pl.pallas_call(
        turn_kernel,
        out_shape=jax.ShapeDtypeStruct((4, states, 2 * width), BF16),
        in_specs=[vmem] * 4,
        out_specs=vmem,
        compiler_params=pltpu.CompilerParams(vmem_limit_bytes=4 * 1024 * 1024),
        interpret=INTERPRET,
        name="turn",
    )(own, *others)


def half_kernel(got, out):
    out[...] = jnp.sum(got[...].astype(F32), axis=0).T.astype(BF16)


def end_kernel(got, out):
    out[...] = jnp.sum(got[...].astype(F32), axis=0)


def small(body, value, out_shape):
    vmem = pl.BlockSpec(memory_space=pltpu.VMEM)
    return pl.pallas_call(
        body,
        out_shape=out_shape,
        in_specs=[vmem],
        out_specs=vmem,
        compiler_params=pltpu.CompilerParams(vmem_limit_bytes=8 * 1024 * 1024),
        interpret=INTERPRET,
    )(value)


def on_device(elements, strength, pole_freq, energies, imag_freqs):
    band_count, row_count, states = elements.shape
    width = strength.shape[1]
    z = lax.axis_index("z")
    yl = lax.axis_index("yl")
    c = lax.axis_index("c")
    yh = lax.axis_index("yh")
    x = lax.axis_index("x")
    total_rows = row_count * 8
    scale = 1.0 / (total_rows * math.sqrt(band_count * 32))

    combos = ((0, 0), (0, 1), (1, 0), (1, 1))
    starts = jnp.stack([((yl ^ a) * 2 + (yh ^ b)) * width for a, b in combos]).astype(jnp.int32)
    out = []
    for slot in (0, -1, 1, -2, 2, 0, -3, 3, 4):
        block = (z + slot) % 8
        out += [(block % 4 - x) % 4, (block // 4) ^ yh]
    out += [yh ^ (pair % 2) ^ c for pair in range(4)]
    where = jnp.stack(out).astype(jnp.int32)

    screen, own, *sent, tall = front(starts, where, energies, strength, pole_freq, elements)

    held = move(screen, ("c", "yh"), lambda cc, hh: (hh, cc))

    others = [
        move(value, ("yl", "yh"), functools.partial(lambda a, b, l, h: (l ^ a, h ^ b), a, b))
        for (a, b), value in zip(combos[1:], sent)
    ]

    rows = []
    for a in range(2):
        for b in range(2):
            target = functools.partial(lambda a, b, l, cc, h: (l ^ a, h, cc ^ b), a, b)
            rows.append(move(tall, ("yl", "c", "yh"), target))

    up, down = held, held
    pieces = {0: held}
    for step in range(1, 4):
        up = move(up, ("z",), lambda i: (i + 1,))
        down = move(down, ("z",), lambda i: (i - 1,))
        pieces[-step], pieces[step] = up, down
    last_up = move(up[0], ("z",), lambda i: (i + 1,))
    last_down = move(down[1], ("z",), lambda i: (i - 1,))

    turned = turn(own, others)
    by_x = [
        turned,
        move(turned, ("x",), lambda i: (i - 1,)),
        move(turned, ("x",), lambda i: (i + 2,)),
        move(turned, ("x",), lambda i: (i + 1,)),
    ]
    columns = []
    for value in by_x:
        columns.append(value)
        columns.append(move(value, ("c",), lambda i: (i ^ 1,)))

    parts, kept = early_sum(imag_freqs, [pieces[s] for s in (0, -1, 1, -2, 2)], rows)
    flat = [pieces[-3], pieces[3], last_up, last_down]
    blocks = late_sum(scale, where, imag_freqs, kept, parts, flat, columns)
    got = lax.all_to_all(blocks, PW, 0, 0, tiled=True)
    part = small(half_kernel, got, jax.ShapeDtypeStruct((states, states // 4), BF16))
    part = lax.all_to_all(part.reshape(32, states // 32, states // 4), BAND, 0, 0, tiled=True)
    done = small(end_kernel, part, jax.ShapeDtypeStruct((states // 32, states // 4), F32))
    return done.reshape(states // 32, 2, states // 8).transpose(1, 0, 2)


def solution(mesh):
    fine = Mesh(mesh.devices.reshape(8, 2, 2, 2, 4), ("z", "yl", "c", "yh", "x"))
    in_specs = (P(BAND, PW, None), P(PW, BAND), P(PW, BAND), P(BAND), P())
    out_specs = P(None, BAND, PW)
    return jax.shard_map(
        on_device, mesh=fine, in_specs=in_specs, out_specs=out_specs, check_vma=False
    )
```

```python
import functools
import math

import jax
import jax.numpy as jnp
from jax import lax
from jax.experimental import pallas as pl
from jax.experimental.pallas import tpu as pltpu
from jax.sharding import Mesh
from jax.sharding import PartitionSpec as P


INTERPRET = False
FRONT_VMEM = 64 * 1024 * 1024 - 1600 * 1024

SIZES = {"z": 8, "yl": 2, "c": 2, "yh": 2, "x": 4}
BAND = ("z", "yl", "c")
PW = ("yh", "x")
F32 = jnp.float32
BF16 = jnp.bfloat16


def move(value, axes, target):
    sizes = [SIZES[axis] for axis in axes]
    total = math.prod(sizes)

    def flat(indices):
        out = 0
        for index, size in zip(indices, sizes):
            out = out * size + index % size
        return out

    pairs = []
    for source in range(total):
        rest, indices = source, []
        for size in reversed(sizes):
            indices.append(rest % size)
            rest //= size
        pairs.append((source, flat(target(*reversed(indices)))))
    return lax.ppermute(value, axes, pairs)


def load(copies, screen, wide):
    for copy in copies:
        copy.wait()
    for slot in range(wide.shape[0]):
        wide[slot] = screen[slot].astype(F32)


def fill(kern, wide, levels, nu, unit):
    slot, pair = unit // 4, unit % 4
    width = wide.shape[2]
    tile = min(16, width)
    for start in range(0, width, tile):
        here = pl.ds(start, tile)
        strength = wide[slot, 0, here, :]
        pole = wide[slot, 1, here, :]
        for k in range(2):
            shifted = pole + levels[2 * pair + k]
            square = shifted * shifted
            above = strength * shifted
            for e in range(2):
                below = square + nu[e] * nu[e]
                kern[k, pl.ds(e * width + start, tile), :] = (
                    above * pl.reciprocal(below)
                ).astype(BF16)


def rows_dot(kern, held, part, unit):
    pair = unit % 4
    width, height = kern.shape[1] // 2, kern.shape[2]
    for k in range(2):
        value = jnp.dot(
            kern[k], held[2 * pair + k, pl.ds(0, height), :], preferred_element_type=F32
        ).astype(BF16)
        part[0, pl.ds(k * width, width), :] = value[:width]
        part[1, pl.ds(k * width, width), :] = value[width:]


def read_levels(held, levels, height):
    for band in range(8):
        parts = held[band, pl.ds(height, 16), :].astype(F32)
        levels[band] = (parts[0:1] + parts[1:2] + parts[2:3])[0, 0]


def piece_of(ref, slot):
    return ref if len(ref.shape) == 3 else ref.at[1 - slot % 2]


def early_kernel(count, *refs):
    nu, pieces, rows = refs[0], refs[1 : 1 + count], refs[1 + count : 3 + count]
    parts, held, screen, wide, kern_a, kern_b, levels, sems = refs[3 + count :]
    height = wide.shape[3]
    copies = [
        pltpu.make_async_copy(piece_of(pieces[slot], slot), screen.at[slot], sems.at[slot])
        for slot in range(count)
    ]
    for copy in copies:
        copy.start()
    for pair in range(4):
        for k in range(2):
            held[2 * pair + k] = rows[pair // 2][pair % 2, k]
    read_levels(held, levels, height)
    load(copies, screen, wide)
    last = 4 * count - 1
    fill(kern_a, wide, levels, nu, 0)

    def four(step, carry):
        for unit in (4 * step, 4 * step + 2):
            fill(kern_b, wide, levels, nu, unit + 1)
            rows_dot(kern_a, held, parts.at[unit], unit)
            fill(kern_a, wide, levels, nu, jnp.minimum(unit + 2, last))
            rows_dot(kern_b, held, parts.at[unit + 1], unit + 1)
        return carry

    lax.fori_loop(0, count, four, 0)
    for unit in range(4 * count, parts.shape[0]):
        parts[unit] = jnp.zeros_like(parts[unit])


def late_kernel(count, scale, *refs):
    where, nu, held, early = refs[:4]
    flat = refs[4 : 4 + count]
    mine, theirs, near, far, across0, across1 = refs[4 + count : 10 + count]
    out, screen, wide, cols, kern_a, kern_b, part_a, part_b, total, levels, sems = refs[10 + count :]
    height = wide.shape[3]
    copies = [
        pltpu.make_async_copy(piece_of(flat[slot], slot + 1), screen.at[slot], sems.at[slot])
        for slot in range(count)
    ]
    for copy in copies:
        copy.start()
    for other in range(2):
        cols[0, other] = (mine, theirs)[other][...]
        cols[1, other] = near[other]
        cols[2, other] = (across0, across1)[other][...]
        cols[3, other] = far[1 - other]
    total[...] = jnp.zeros_like(total)
    part_b[...] = jnp.zeros_like(part_b)
    read_levels(held, levels, height)
    load(copies, screen, wide)
    last = 4 * count - 1

    def columns_dot(part, slot, unit):
        pair = unit % 4
        left = cols[where[2 * slot], where[18 + pair], pair // 2 * 2 + where[2 * slot + 1]]
        total[0] += jnp.dot(left, part[0], preferred_element_type=F32)
        total[1] += jnp.dot(left, part[1], preferred_element_type=F32)

    fill(kern_a, wide, levels, nu, 0)

    def early_dots(unit):
        for other in (2 * unit, 2 * unit + 1):
            columns_dot(early.at[other], other // 4, other)

    def four(step, carry):
        for unit in (4 * step, 4 * step + 2):
            before = jnp.maximum(unit - 1, 0)
            fill(kern_b, wide, levels, nu, unit + 1)
            rows_dot(kern_a, held, part_a, unit)
            early_dots(unit)
            columns_dot(part_b, 6 + before // 4, before)
            fill(kern_a, wide, levels, nu, jnp.minimum(unit + 2, last))
            rows_dot(kern_b, held, part_b, unit + 1)
            early_dots(unit + 1)
            columns_dot(part_a, 6 + unit // 4, unit)
        return carry

    lax.fori_loop(0, count, four, 0)
    columns_dot(part_b, 6 + last // 4, last)
    blocks, tall = out.shape[0], out.shape[1] // 2
    for block in range(blocks):
        for e in range(2):
            out[block, pl.ds(e * tall, tall), :] = (
                total[e, pl.ds(block * tall, tall), :] * scale
            ).astype(BF16)


SMEM = pl.BlockSpec(memory_space=pltpu.SMEM)
VMEM = pl.BlockSpec(memory_space=pltpu.VMEM)
ANY = pl.BlockSpec(memory_space=pl.ANY)


def screen_scratch(count, width, height):
    return [
        pltpu.VMEM((count, 2, width, height), BF16),
        pltpu.VMEM((count, 2, width, height), F32),
    ]


def early_sum(nu, pieces, rows):
    count = len(pieces)
    _, width, height = pieces[0].shape
    states = rows[0].shape[3]
    kern = pltpu.VMEM((2, 2 * width, height), BF16)
    flops = count * 8 * 2 * 2 * width * height * states
    return pl.pallas_call(
        functools.partial(early_kernel, count),
        out_shape=(
            jax.ShapeDtypeStruct((24, 2, 2 * width, states), BF16),
            jax.ShapeDtypeStruct((8, height + 16, states), BF16),
        ),
        in_specs=[SMEM] + [ANY] * count + [VMEM] * 2,
        out_specs=(VMEM, VMEM),
        scratch_shapes=screen_scratch(count, width, height)
        + [kern, kern, pltpu.SMEM((8,), F32), pltpu.SemaphoreType.DMA((count,))],
        compiler_params=pltpu.CompilerParams(vmem_limit_bytes=16 * 1024 * 1024),
        cost_estimate=pl.CostEstimate(
            flops=flops,
            bytes_accessed=8 * 1024 * 1024,
            transcendentals=count * 16 * width * height,
        ),
        interpret=INTERPRET,
        name="early_sum",
    )(nu, *pieces, *rows)


def late_sum(scale, where, nu, held, early, flat, columns):
    count = len(flat)
    _, width, height = flat[-1].shape
    states = held.shape[2]
    kern = pltpu.VMEM((2, 2 * width, height), BF16)
    part = pltpu.VMEM((2, 2 * width, states), BF16)
    flops = count * 8 * 2 * 2 * (width * height * states + 3 * width * states * states)
    return pl.pallas_call(
        functools.partial(late_kernel, count, scale),
        out_shape=jax.ShapeDtypeStruct((8, states // 4, states), BF16),
        in_specs=[SMEM] * 2 + [VMEM] * 2 + [ANY] * count + [VMEM] * 6,
        out_specs=VMEM,
        scratch_shapes=screen_scratch(count, width, height)
        + [pltpu.VMEM((4, 2) + columns[0].shape, BF16), kern, kern, part, part]
        + [pltpu.VMEM((2, states, states), F32), pltpu.SMEM((8,), F32)]
        + [pltpu.SemaphoreType.DMA((count,))],
        compiler_params=pltpu.CompilerParams(vmem_limit_bytes=20 * 1024 * 1024),
        cost_estimate=pl.CostEstimate(
            flops=flops,
            bytes_accessed=8 * 1024 * 1024,
            transcendentals=count * 16 * width * height,
        ),
        interpret=INTERPRET,
        name="late_sum",
    )(where, nu, held, early, *flat, *columns)


def front_kernel(starts, where, energies, strength, pole, elements, *refs):
    screen, own, part01, part10, part11, tall, loaded, sems = refs
    height, width = strength.shape
    copies = [
        pltpu.make_async_copy(strength, loaded.at[0], sems.at[0]),
        pltpu.make_async_copy(pole, loaded.at[1], sems.at[1]),
        pltpu.make_async_copy(elements, tall.at[:, pl.ds(0, height), :], sems.at[2]),
    ]
    for copy in copies:
        copy.start()
    shape = (16, tall.shape[2])
    line = lax.broadcasted_iota(jnp.int32, shape, 0)
    for k in range(2):
        level = jnp.full(shape, energies[k], F32)
        high = level.astype(BF16).astype(F32)
        middle = (level - high).astype(BF16).astype(F32)
        low = level - high - middle
        value = jnp.where(line == 0, high, jnp.where(line == 1, middle, low))
        tall[k, pl.ds(height, 16), :] = value.astype(BF16)
    copies[0].wait()
    copies[1].wait()
    for part in range(2):
        screen[part] = loaded[part].T
    copies[2].wait()
    for slot, out in enumerate((own, part01, part10, part11)):
        out[...] = tall[:, pl.ds(pl.multiple_of(starts[slot], width), width), :]


def front(starts, where, energies, strength, pole, elements):
    height, width = strength.shape
    states = elements.shape[2]
    smem = pl.BlockSpec(memory_space=pltpu.SMEM)
    vmem = pl.BlockSpec(memory_space=pltpu.VMEM)
    anywhere = pl.BlockSpec(memory_space=pltpu.HBM)
    piece = jax.ShapeDtypeStruct((2, width, states), BF16)
    return pl.pallas_call(
        front_kernel,
        out_shape=(
            jax.ShapeDtypeStruct((2, width, height), BF16),
            piece,
            piece,
            piece,
            piece,
            jax.ShapeDtypeStruct((2, height + 16, states), BF16),
        ),
        in_specs=[smem] * 3 + [anywhere] * 3,
        out_specs=(vmem,) * 6,
        scratch_shapes=[pltpu.VMEM((2, height, width), BF16), pltpu.SemaphoreType.DMA((3,))],
        compiler_params=pltpu.CompilerParams(vmem_limit_bytes=FRONT_VMEM),
        interpret=INTERPRET,
        name="front",
    )(starts, where, energies, strength, pole, elements)


def turn_kernel(own, other0, other1, other2, out):
    width, states = own.shape[1:]
    for slot, ref in enumerate((own, other0, other1, other2)):
        out[slot] = ref[...].reshape(2 * width, states).T


def turn(own, others):
    width, states = own.shape[1:]
    vmem = pl.BlockSpec(memory_space=pltpu.VMEM)
    return pl.pallas_call(
        turn_kernel,
        out_shape=jax.ShapeDtypeStruct((4, states, 2 * width), BF16),
        in_specs=[vmem] * 4,
        out_specs=vmem,
        compiler_params=pltpu.CompilerParams(vmem_limit_bytes=4 * 1024 * 1024),
        interpret=INTERPRET,
        name="turn",
    )(own, *others)


def pair_kernel(first, second, out):
    out[0] = first[...]
    out[1] = second[...]


def pair_up(first, second):
    vmem = pl.BlockSpec(memory_space=pltpu.VMEM)
    return pl.pallas_call(
        pair_kernel,
        out_shape=jax.ShapeDtypeStruct((2,) + first.shape, first.dtype),
        in_specs=[vmem] * 2,
        out_specs=vmem,
        compiler_params=pltpu.CompilerParams(vmem_limit_bytes=4 * 1024 * 1024),
        interpret=INTERPRET,
    )(first, second)


def half_kernel(got, out):
    out[...] = jnp.sum(got[...].astype(F32), axis=0).T.astype(BF16)


def end_kernel(got, out):
    out[...] = jnp.sum(got[...].astype(F32), axis=0)


def small(body, value, out_shape):
    vmem = pl.BlockSpec(memory_space=pltpu.VMEM)
    return pl.pallas_call(
        body,
        out_shape=out_shape,
        in_specs=[vmem],
        out_specs=vmem,
        compiler_params=pltpu.CompilerParams(vmem_limit_bytes=8 * 1024 * 1024),
        interpret=INTERPRET,
    )(value)


def on_device(elements, strength, pole_freq, energies, imag_freqs):
    band_count, row_count, states = elements.shape
    width = strength.shape[1]
    z = lax.axis_index("z")
    yl = lax.axis_index("yl")
    c = lax.axis_index("c")
    yh = lax.axis_index("yh")
    x = lax.axis_index("x")
    total_rows = row_count * 8
    scale = 1.0 / (total_rows * math.sqrt(band_count * 32))

    combos = ((0, 0), (0, 1), (1, 0), (1, 1))
    starts = jnp.stack([((yl ^ a) * 2 + (yh ^ b)) * width for a, b in combos]).astype(jnp.int32)
    out = []
    side = 1 - 2 * c
    for slot in (0, -1, 1, -2, 2, 0, -3, 3, 4):
        block = (z + slot * side) % 8
        out += [(block % 4 - x) * side % 4, (block // 4) ^ yh]
    out += [yh ^ (pair % 2) ^ c for pair in range(4)]
    where = jnp.stack(out).astype(jnp.int32)

    screen, own, *sent, tall = front(starts, where, energies, strength, pole_freq, elements)

    held = move(screen, ("c", "yh"), lambda cc, hh: (hh, cc))

    others = [
        move(value, ("yl", "yh"), functools.partial(lambda a, b, l, h: (l ^ a, h ^ b), a, b))
        for (a, b), value in zip(combos[1:], sent)
    ]

    flip = lambda i: (i ^ 1,)
    both = pair_up(tall, move(tall, ("c",), flip))
    rows = [
        move(both, ("yl", "c", "yh"), functools.partial(lambda a, l, cc, h: (l ^ a, h, cc), a))
        for a in range(2)
    ]

    ahead = lambda i, cc: (i + 1 - 2 * cc, cc)
    moved = pair_up(held, move(held, ("c",), flip))
    pieces = [held]
    for _ in range(1, 4):
        moved = move(moved, ("z", "c"), ahead)
        pieces += [moved, move(moved, ("c",), flip)]
    pieces.append(move(moved[0], ("z", "c"), ahead))

    turned = turn(own, others)
    theirs = move(turned, ("c",), flip)
    behind = lambda cc, i: (cc, i - 1 + 2 * cc)
    near = move(pair_up(turned, theirs), ("c", "x"), behind)
    across = move(near[0], ("c", "x"), behind)
    columns = (turned, theirs, near, move(near, ("c",), flip), across, move(across, ("c",), flip))

    parts, kept = early_sum(imag_freqs, pieces[:5], rows)
    blocks = late_sum(scale, where, imag_freqs, kept, parts, pieces[5:], columns)
    got = lax.all_to_all(blocks, PW, 0, 0, tiled=True)
    part = small(half_kernel, got, jax.ShapeDtypeStruct((states, states // 4), BF16))
    part = lax.all_to_all(part.reshape(32, states // 32, states // 4), BAND, 0, 0, tiled=True)
    done = small(end_kernel, part, jax.ShapeDtypeStruct((states // 32, states // 4), F32))
    return done.reshape(states // 32, 2, states // 8).transpose(1, 0, 2)


def solution(mesh):
    fine = Mesh(mesh.devices.reshape(8, 2, 2, 2, 4), ("z", "yl", "c", "yh", "x"))
    in_specs = (P(BAND, PW, None), P(PW, BAND), P(PW, BAND), P(BAND), P())
    out_specs = P(None, BAND, PW)
    return jax.shard_map(
        on_device, mesh=fine, in_specs=in_specs, out_specs=out_specs, check_vma=False
    )
```

```python
import functools
import math

import jax
import jax.numpy as jnp
from jax import lax
from jax.experimental import pallas as pl
from jax.experimental.pallas import tpu as pltpu
from jax.sharding import Mesh
from jax.sharding import PartitionSpec as P


INTERPRET = False
SCREEN_VMEM = 64 * 1024 * 1024 - 400 * 1024
ROWS_VMEM = 64 * 1024 * 1024 - 1600 * 1024

SIZES = {"z": 8, "yl": 2, "c": 2, "yh": 2, "x": 4}
BAND = ("z", "yl", "c")
PW = ("yh", "x")
F32 = jnp.float32
BF16 = jnp.bfloat16


def move(value, axes, target):
    sizes = [SIZES[axis] for axis in axes]
    total = math.prod(sizes)

    def flat(indices):
        out = 0
        for index, size in zip(indices, sizes):
            out = out * size + index % size
        return out

    pairs = []
    for source in range(total):
        rest, indices = source, []
        for size in reversed(sizes):
            indices.append(rest % size)
            rest //= size
        pairs.append((source, flat(target(*reversed(indices)))))
    return lax.ppermute(value, axes, pairs)


def load(copies, screen, wide):
    for copy in copies:
        copy.wait()
    for slot in range(wide.shape[0]):
        wide[slot] = screen[slot].astype(F32)


def fill(kern, wide, levels, nu, unit):
    slot, pair = unit // 4, unit % 4
    width = wide.shape[2]
    tile = min(16, width)
    for start in range(0, width, tile):
        here = pl.ds(start, tile)
        strength = wide[slot, 0, here, :]
        pole = wide[slot, 1, here, :]
        for k in range(2):
            shifted = pole + levels[2 * pair + k]
            square = shifted * shifted
            above = strength * shifted
            for e in range(2):
                below = square + nu[e] * nu[e]
                kern[k, pl.ds(e * width + start, tile), :] = (
                    above * pl.reciprocal(below)
                ).astype(BF16)


def rows_dot(kern, held, part, unit):
    pair = unit % 4
    width, height = kern.shape[1] // 2, kern.shape[2]
    for k in range(2):
        value = jnp.dot(
            kern[k], held[2 * pair + k, pl.ds(0, height), :], preferred_element_type=F32
        ).astype(BF16)
        part[0, pl.ds(k * width, width), :] = value[:width]
        part[1, pl.ds(k * width, width), :] = value[width:]


def read_levels(held, levels, height):
    for band in range(8):
        parts = held[band, pl.ds(height, 16), :].astype(F32)
        levels[band] = (parts[0:1] + parts[1:2] + parts[2:3])[0, 0]


def piece_of(ref, slot):
    return ref if len(ref.shape) == 3 else ref.at[1 - slot % 2]


def early_kernel(count, *refs):
    nu, pieces, rows = refs[0], refs[1 : 1 + count], refs[1 + count : 3 + count]
    parts, held, screen, wide, kern_a, kern_b, levels, sems = refs[3 + count :]
    height = wide.shape[3]
    copies = [
        pltpu.make_async_copy(piece_of(pieces[slot], slot), screen.at[slot], sems.at[slot])
        for slot in range(count)
    ]
    for copy in copies:
        copy.start()
    for pair in range(4):
        for k in range(2):
            held[2 * pair + k] = rows[pair // 2][pair % 2, k]
    read_levels(held, levels, height)
    load(copies, screen, wide)
    last = 4 * count - 1
    fill(kern_a, wide, levels, nu, 0)

    def four(step, carry):
        for unit in (4 * step, 4 * step + 2):
            fill(kern_b, wide, levels, nu, unit + 1)
            rows_dot(kern_a, held, parts.at[unit], unit)
            fill(kern_a, wide, levels, nu, jnp.minimum(unit + 2, last))
            rows_dot(kern_b, held, parts.at[unit + 1], unit + 1)
        return carry

    lax.fori_loop(0, count, four, 0)
    for unit in range(4 * count, parts.shape[0]):
        parts[unit] = jnp.zeros_like(parts[unit])


def late_kernel(count, scale, *refs):
    nu, held, early = refs[:3]
    flat = refs[3 : 3 + count]
    mine, theirs, near, far, across0, across1 = refs[3 + count : 9 + count]
    out, screen, wide, cols, kern_a, kern_b, part_a, part_b, total, levels, where, sems = refs[9 + count :]
    height = wide.shape[3]
    copies = [
        pltpu.make_async_copy(piece_of(flat[slot], slot + 1), screen.at[slot], sems.at[slot])
        for slot in range(count)
    ]
    for copy in copies:
        copy.start()
    for other in range(2):
        cols[0, other] = (mine, theirs)[other][...]
        cols[1, other] = near[other]
        cols[2, other] = (across0, across1)[other][...]
        cols[3, other] = far[1 - other]
    z, yh, x, c = (lax.axis_index(axis) for axis in ("z", "yh", "x", "c"))
    side = 1 - 2 * c
    for slot, step in enumerate((0, -1, 1, -2, 2, 0, -3, 3, 4)):
        block = (z + step * side) & 7
        where[2 * slot] = ((block & 3) - x) * side & 3
        where[2 * slot + 1] = (block >> 2) ^ yh
    for pair in range(4):
        where[18 + pair] = yh ^ (pair % 2) ^ c
    total[...] = jnp.zeros_like(total)
    part_b[...] = jnp.zeros_like(part_b)
    read_levels(held, levels, height)
    load(copies, screen, wide)
    last = 4 * count - 1

    def columns_dot(part, slot, unit):
        pair = unit % 4
        left = cols[where[2 * slot], where[18 + pair], pair // 2 * 2 + where[2 * slot + 1]]
        total[0] += jnp.dot(left, part[0], preferred_element_type=F32)
        total[1] += jnp.dot(left, part[1], preferred_element_type=F32)

    fill(kern_a, wide, levels, nu, 0)

    def early_dots(unit):
        for other in (2 * unit, 2 * unit + 1):
            columns_dot(early.at[other], other // 4, other)

    def four(step, carry):
        for unit in (4 * step, 4 * step + 2):
            before = jnp.maximum(unit - 1, 0)
            fill(kern_b, wide, levels, nu, unit + 1)
            rows_dot(kern_a, held, part_a, unit)
            early_dots(unit)
            columns_dot(part_b, 6 + before // 4, before)
            fill(kern_a, wide, levels, nu, jnp.minimum(unit + 2, last))
            rows_dot(kern_b, held, part_b, unit + 1)
            early_dots(unit + 1)
            columns_dot(part_a, 6 + unit // 4, unit)
        return carry

    lax.fori_loop(0, count, four, 0)
    columns_dot(part_b, 6 + last // 4, last)
    blocks, tall = out.shape[0], out.shape[1] // 2
    for block in range(blocks):
        for e in range(2):
            out[block, pl.ds(e * tall, tall), :] = (
                total[e, pl.ds(block * tall, tall), :] * scale
            ).astype(BF16)


SMEM = pl.BlockSpec(memory_space=pltpu.SMEM)
VMEM = pl.BlockSpec(memory_space=pltpu.VMEM)
ANY = pl.BlockSpec(memory_space=pl.ANY)


def screen_scratch(count, width, height):
    return [
        pltpu.VMEM((count, 2, width, height), BF16),
        pltpu.VMEM((count, 2, width, height), F32),
    ]


def early_sum(nu, pieces, rows):
    count = len(pieces)
    _, width, height = pieces[0].shape
    states = rows[0].shape[3]
    kern = pltpu.VMEM((2, 2 * width, height), BF16)
    flops = count * 8 * 2 * 2 * width * height * states
    return pl.pallas_call(
        functools.partial(early_kernel, count),
        out_shape=(
            jax.ShapeDtypeStruct((24, 2, 2 * width, states), BF16),
            jax.ShapeDtypeStruct((8, height + 16, states), BF16),
        ),
        in_specs=[SMEM] + [ANY] * count + [VMEM] * 2,
        out_specs=(VMEM, VMEM),
        scratch_shapes=screen_scratch(count, width, height)
        + [kern, kern, pltpu.SMEM((8,), F32), pltpu.SemaphoreType.DMA((count,))],
        compiler_params=pltpu.CompilerParams(vmem_limit_bytes=16 * 1024 * 1024),
        cost_estimate=pl.CostEstimate(
            flops=flops,
            bytes_accessed=8 * 1024 * 1024,
            transcendentals=count * 16 * width * height,
        ),
        interpret=INTERPRET,
        name="early_sum",
    )(nu, *pieces, *rows)


def late_sum(scale, nu, held, early, flat, columns):
    count = len(flat)
    _, width, height = flat[-1].shape
    states = held.shape[2]
    kern = pltpu.VMEM((2, 2 * width, height), BF16)
    part = pltpu.VMEM((2, 2 * width, states), BF16)
    flops = count * 8 * 2 * 2 * (width * height * states + 3 * width * states * states)
    return pl.pallas_call(
        functools.partial(late_kernel, count, scale),
        out_shape=jax.ShapeDtypeStruct((8, states // 4, states), BF16),
        in_specs=[SMEM] + [VMEM] * 2 + [ANY] * count + [VMEM] * 6,
        out_specs=VMEM,
        scratch_shapes=screen_scratch(count, width, height)
        + [pltpu.VMEM((4, 2) + columns[0].shape, BF16), kern, kern, part, part]
        + [pltpu.VMEM((2, states, states), F32), pltpu.SMEM((8,), F32)]
        + [pltpu.SMEM((22,), jnp.int32)]
        + [pltpu.SemaphoreType.DMA((count,))],
        compiler_params=pltpu.CompilerParams(vmem_limit_bytes=20 * 1024 * 1024),
        cost_estimate=pl.CostEstimate(
            flops=flops,
            bytes_accessed=8 * 1024 * 1024,
            transcendentals=count * 16 * width * height,
        ),
        interpret=INTERPRET,
        name="late_sum",
    )(nu, held, early, *flat, *columns)


def screen_kernel(strength, pole, out, loaded, sems):
    copies = [
        pltpu.make_async_copy(strength, loaded.at[0], sems.at[0]),
        pltpu.make_async_copy(pole, loaded.at[1], sems.at[1]),
    ]
    for copy in copies:
        copy.start()
    for part, copy in enumerate(copies):
        copy.wait()
        out[part] = loaded[part].T


def front_screen(strength, pole):
    height, width = strength.shape
    return pl.pallas_call(
        screen_kernel,
        out_shape=jax.ShapeDtypeStruct((2, width, height), BF16),
        in_specs=[ANY] * 2,
        out_specs=VMEM,
        scratch_shapes=[pltpu.VMEM((2, height, width), BF16), pltpu.SemaphoreType.DMA((2,))],
        compiler_params=pltpu.CompilerParams(vmem_limit_bytes=SCREEN_VMEM),
        interpret=INTERPRET,
        name="front_screen",
    )(strength, pole)


def rows_kernel(energies, elements, own, part01, part10, part11, tall, sem):
    height, width = elements.shape[1], own.shape[1]
    copy = pltpu.make_async_copy(elements, tall.at[:, pl.ds(0, height), :], sem.at[0])
    copy.start()
    shape = (16, tall.shape[2])
    line = lax.broadcasted_iota(jnp.int32, shape, 0)
    for k in range(2):
        level = jnp.full(shape, energies[k], F32)
        high = level.astype(BF16).astype(F32)
        middle = (level - high).astype(BF16).astype(F32)
        low = level - high - middle
        value = jnp.where(line == 0, high, jnp.where(line == 1, middle, low))
        tall[k, pl.ds(height, 16), :] = value.astype(BF16)
    yl, yh = lax.axis_index("yl"), lax.axis_index("yh")
    copy.wait()
    for slot, out in enumerate((own, part01, part10, part11)):
        piece = (yl ^ (slot // 2)) * 2 + (yh ^ (slot % 2))
        out[...] = tall[:, pl.ds(pl.multiple_of(piece * width, width), width), :]


def front_rows(energies, elements, width):
    _, height, states = elements.shape
    piece = jax.ShapeDtypeStruct((2, width, states), BF16)
    return pl.pallas_call(
        rows_kernel,
        out_shape=(piece,) * 4 + (jax.ShapeDtypeStruct((2, height + 16, states), BF16),),
        in_specs=[SMEM, ANY],
        out_specs=(VMEM,) * 5,
        scratch_shapes=[pltpu.SemaphoreType.DMA((1,))],
        compiler_params=pltpu.CompilerParams(vmem_limit_bytes=ROWS_VMEM),
        interpret=INTERPRET,
        name="front_rows",
    )(energies, elements)


def turn_kernel(own, other0, other1, other2, out):
    width, states = own.shape[1:]
    for slot, ref in enumerate((own, other0, other1, other2)):
        out[slot] = ref[...].reshape(2 * width, states).T


def turn(own, others):
    width, states = own.shape[1:]
    vmem = pl.BlockSpec(memory_space=pltpu.VMEM)
    return pl.pallas_call(
        turn_kernel,
        out_shape=jax.ShapeDtypeStruct((4, states, 2 * width), BF16),
        in_specs=[vmem] * 4,
        out_specs=vmem,
        compiler_params=pltpu.CompilerParams(vmem_limit_bytes=4 * 1024 * 1024),
        interpret=INTERPRET,
        name="turn",
    )(own, *others)


def pair_kernel(first, second, out):
    out[0] = first[...]
    out[1] = second[...]


def pair_up(first, second):
    vmem = pl.BlockSpec(memory_space=pltpu.VMEM)
    return pl.pallas_call(
        pair_kernel,
        out_shape=jax.ShapeDtypeStruct((2,) + first.shape, first.dtype),
        in_specs=[vmem] * 2,
        out_specs=vmem,
        compiler_params=pltpu.CompilerParams(vmem_limit_bytes=4 * 1024 * 1024),
        interpret=INTERPRET,
    )(first, second)


def half_kernel(got, out):
    out[...] = jnp.sum(got[...].astype(F32), axis=0).T.astype(BF16)


def end_kernel(got, out):
    value = jnp.sum(got[...].astype(F32), axis=0)
    half = value.shape[1] // 2
    out[0] = value[:, :half]
    out[1] = value[:, half:]


def small(body, value, out_shape):
    vmem = pl.BlockSpec(memory_space=pltpu.VMEM)
    return pl.pallas_call(
        body,
        out_shape=out_shape,
        in_specs=[vmem],
        out_specs=vmem,
        compiler_params=pltpu.CompilerParams(vmem_limit_bytes=8 * 1024 * 1024),
        interpret=INTERPRET,
    )(value)


def on_device(elements, strength, pole_freq, energies, imag_freqs):
    band_count, row_count, states = elements.shape
    width = strength.shape[1]
    total_rows = row_count * 8
    scale = 1.0 / (total_rows * math.sqrt(band_count * 32))

    combos = ((0, 0), (0, 1), (1, 0), (1, 1))
    screen = front_screen(strength, pole_freq)
    own, *sent, tall = front_rows(energies, elements, width)

    held = move(screen, ("c", "yh"), lambda cc, hh: (hh, cc))

    others = [
        move(value, ("yl", "yh"), functools.partial(lambda a, b, l, h: (l ^ a, h ^ b), a, b))
        for (a, b), value in zip(combos[1:], sent)
    ]

    flip = lambda i: (i ^ 1,)
    both = pair_up(tall, move(tall, ("c",), flip))
    rows = [
        move(both, ("yl", "c", "yh"), functools.partial(lambda a, l, cc, h: (l ^ a, h, cc), a))
        for a in range(2)
    ]

    ahead = lambda i, cc: (i + 1 - 2 * cc, cc)
    moved = pair_up(held, move(held, ("c",), flip))
    pieces = [held]
    for _ in range(1, 4):
        moved = move(moved, ("z", "c"), ahead)
        pieces += [moved, move(moved, ("c",), flip)]
    pieces.append(move(moved[0], ("z", "c"), ahead))

    turned = turn(own, others)
    theirs = move(turned, ("c",), flip)
    behind = lambda cc, i: (cc, i - 1 + 2 * cc)
    near = move(pair_up(turned, theirs), ("c", "x"), behind)
    across = move(near[0], ("c", "x"), behind)
    columns = (turned, theirs, near, move(near, ("c",), flip), across, move(across, ("c",), flip))

    parts, kept = early_sum(imag_freqs, pieces[:5], rows)
    blocks = late_sum(scale, imag_freqs, kept, parts, pieces[5:], columns)
    got = lax.all_to_all(blocks, PW, 0, 0, tiled=True)
    part = small(half_kernel, got, jax.ShapeDtypeStruct((states, states // 4), BF16))
    part = lax.all_to_all(part.reshape(32, states // 32, states // 4), BAND, 0, 0, tiled=True)
    return small(end_kernel, part, jax.ShapeDtypeStruct((2, states // 32, states // 8), F32))


def solution(mesh):
    fine = Mesh(mesh.devices.reshape(8, 2, 2, 2, 4), ("z", "yl", "c", "yh", "x"))
    in_specs = (P(BAND, PW, None), P(PW, BAND), P(PW, BAND), P(BAND), P())
    out_specs = P(None, BAND, PW)
    return jax.shard_map(
        on_device, mesh=fine, in_specs=in_specs, out_specs=out_specs, check_vma=False
    )
```

```python
import functools
import math

import jax
import jax.numpy as jnp
from jax import lax
from jax.experimental import pallas as pl
from jax.experimental.pallas import tpu as pltpu
from jax.sharding import Mesh
from jax.sharding import PartitionSpec as P


INTERPRET = False
SCREEN_VMEM = 64 * 1024 * 1024 - 400 * 1024
ROWS_VMEM = 64 * 1024 * 1024 - 1600 * 1024

SIZES = {"z": 8, "yl": 2, "c": 2, "yh": 2, "x": 4}
BAND = ("z", "yl", "c")
PW = ("yh", "x")
F32 = jnp.float32
BF16 = jnp.bfloat16


def move(value, axes, target):
    sizes = [SIZES[axis] for axis in axes]
    total = math.prod(sizes)

    def flat(indices):
        out = 0
        for index, size in zip(indices, sizes):
            out = out * size + index % size
        return out

    pairs = []
    for source in range(total):
        rest, indices = source, []
        for size in reversed(sizes):
            indices.append(rest % size)
            rest //= size
        pairs.append((source, flat(target(*reversed(indices)))))
    return lax.ppermute(value, axes, pairs)


def load(copies, screen, wide):
    for copy in copies:
        copy.wait()
    for slot in range(wide.shape[0]):
        wide[slot] = screen[slot].astype(F32)


def fill(kern, wide, levels, nu, unit):
    slot, pair = unit // 4, unit % 4
    width = wide.shape[2]
    tile = min(16, width)
    for start in range(0, width, tile):
        here = pl.ds(start, tile)
        strength = wide[slot, 0, here, :]
        pole = wide[slot, 1, here, :]
        for k in range(2):
            shifted = pole + levels[2 * pair + k]
            square = shifted * shifted
            above = strength * shifted
            for e in range(2):
                below = square + nu[e] * nu[e]
                kern[k, pl.ds(e * width + start, tile), :] = (
                    above * pl.reciprocal(below)
                ).astype(BF16)


def rows_dot(kern, held, part, unit):
    pair = unit % 4
    width, height = kern.shape[1] // 2, kern.shape[2]
    for k in range(2):
        value = jnp.dot(
            kern[k], held[2 * pair + k, pl.ds(0, height), :], preferred_element_type=F32
        ).astype(BF16)
        part[0, pl.ds(k * width, width), :] = value[:width]
        part[1, pl.ds(k * width, width), :] = value[width:]


def read_levels(held, levels, height):
    for band in range(8):
        parts = held[band, pl.ds(height, 16), :].astype(F32)
        levels[band] = (parts[0:1] + parts[1:2] + parts[2:3])[0, 0]


def piece_copies(pieces, picks, screen, sems):
    copies = []
    for slot, (ref, pick) in enumerate(zip(pieces, picks)):
        source = ref if pick is None else ref.at[pick]
        copies.append(pltpu.make_async_copy(source, screen.at[slot], sems.at[slot]))
    for copy in copies:
        copy.start()
    return copies


def early_kernel(first, picks, *refs):
    count = len(picks)
    nu, pieces, rows = refs[0], refs[1 : 1 + count], refs[1 + count :]
    if first:
        rows, (parts, held, screen, wide, kern_a, kern_b, levels, sems) = rows[:2], rows[2:]
    else:
        held, parts, screen, wide, kern_a, kern_b, levels, sems = rows
    height = wide.shape[3]
    copies = piece_copies(pieces, picks, screen, sems)
    if first:
        for pair in range(4):
            for k in range(2):
                held[2 * pair + k] = rows[pair // 2][pair % 2, k]
    read_levels(held, levels, height)
    load(copies, screen, wide)
    last = 4 * count - 1
    fill(kern_a, wide, levels, nu, 0)

    def four(step, carry):
        for unit in (4 * step, 4 * step + 2):
            fill(kern_b, wide, levels, nu, unit + 1)
            rows_dot(kern_a, held, parts.at[unit], unit)
            fill(kern_a, wide, levels, nu, jnp.minimum(unit + 2, last))
            rows_dot(kern_b, held, parts.at[unit + 1], unit + 1)
        return carry

    lax.fori_loop(0, count, four, 0)


def late_kernel(picks, scale, *refs):
    count = len(picks)
    nu, held = refs[:2]
    early = refs[2 : 2 + count]
    flat = refs[2 + count : 2 + 2 * count]
    mine, theirs, near, far, across0, across1 = refs[2 + 2 * count : 8 + 2 * count]
    out, screen, wide, cols, kern_a, kern_b, part_a, part_b, total, levels, where, sems = refs[
        8 + 2 * count :
    ]
    height = wide.shape[3]
    copies = piece_copies(flat, picks, screen, sems)
    for other in range(2):
        cols[0, other] = (mine, theirs)[other][...]
        cols[1, other] = near[other]
        cols[2, other] = (across0, across1)[other][...]
        cols[3, other] = far[1 - other]
    z, yh, x, c = (lax.axis_index(axis) for axis in ("z", "yh", "x", "c"))
    side = 1 - 2 * c
    for slot, step in enumerate((0, -1, 1, -2, 2, -3, 3, 4)):
        block = (z + step * side) & 7
        where[2 * slot] = ((block & 3) - x) * side & 3
        where[2 * slot + 1] = (block >> 2) ^ yh
    for pair in range(4):
        where[16 + pair] = yh ^ (pair % 2) ^ c
    total[...] = jnp.zeros_like(total)
    read_levels(held, levels, height)
    load(copies, screen, wide)
    units = 4 * count

    def columns_dot(part, slot, unit):
        pair = unit % 4
        left = cols[where[2 * slot], where[16 + pair], pair // 2 * 2 + where[2 * slot + 1]]
        total[0] += jnp.dot(left, part[0], preferred_element_type=F32)
        total[1] += jnp.dot(left, part[1], preferred_element_type=F32)

    fill(kern_a, wide, levels, nu, 0)
    kerns, parts = (kern_a, kern_b), (part_a, part_b)
    for unit in range(units):
        group, inner = unit // 4, unit % 4
        if unit + 1 < units:
            fill(kerns[(unit + 1) % 2], wide, levels, nu, unit + 1)
        rows_dot(kerns[unit % 2], held, parts[unit % 2], unit)
        for other in range(3 * inner, 3 * inner + 3):
            columns_dot(early[group].at[other], 3 * group + other // 4, other)
        if unit:
            columns_dot(parts[(unit - 1) % 2], 6 + (unit - 1) // 4, unit - 1)
    columns_dot(parts[(units - 1) % 2], 6 + (units - 1) // 4, units - 1)
    blocks, tall = out.shape[0], out.shape[1] // 2
    for block in range(blocks):
        for e in range(2):
            out[block, pl.ds(e * tall, tall), :] = (
                total[e, pl.ds(block * tall, tall), :] * scale
            ).astype(BF16)


SMEM = pl.BlockSpec(memory_space=pltpu.SMEM)
VMEM = pl.BlockSpec(memory_space=pltpu.VMEM)
ANY = pl.BlockSpec(memory_space=pl.ANY)


def screen_scratch(count, width, height):
    return [
        pltpu.VMEM((count, 2, width, height), BF16),
        pltpu.VMEM((count, 2, width, height), F32),
    ]


def early_sum(nu, pieces, picks, rows, shape):
    count = len(pieces)
    width, height, states = shape
    first = len(rows) == 2
    kern = pltpu.VMEM((2, 2 * width, height), BF16)
    out_shape = [jax.ShapeDtypeStruct((4 * count, 2, 2 * width, states), BF16)]
    if first:
        out_shape.append(jax.ShapeDtypeStruct((8, height + 16, states), BF16))
    flops = count * 8 * 2 * 2 * width * height * states
    return pl.pallas_call(
        functools.partial(early_kernel, first, picks),
        out_shape=out_shape,
        in_specs=[SMEM] + [ANY] * count + [VMEM] * len(rows),
        out_specs=[VMEM] * len(out_shape),
        scratch_shapes=screen_scratch(count, width, height)
        + [kern, kern, pltpu.SMEM((8,), F32), pltpu.SemaphoreType.DMA((count,))],
        compiler_params=pltpu.CompilerParams(vmem_limit_bytes=12 * 1024 * 1024),
        cost_estimate=pl.CostEstimate(
            flops=flops,
            bytes_accessed=8 * 1024 * 1024,
            transcendentals=count * 16 * width * height,
        ),
        interpret=INTERPRET,
    )(nu, *pieces, *rows)


def late_sum(scale, nu, held, early, flat, picks, columns, shape):
    count = len(flat)
    width, height, states = shape
    kern = pltpu.VMEM((2, 2 * width, height), BF16)
    part = pltpu.VMEM((2, 2 * width, states), BF16)
    flops = count * 8 * 2 * 2 * (width * height * states + 4 * width * states * states)
    return pl.pallas_call(
        functools.partial(late_kernel, picks, scale),
        out_shape=jax.ShapeDtypeStruct((8, states // 4, states), BF16),
        in_specs=[SMEM] + [VMEM] * (1 + count) + [ANY] * count + [VMEM] * 6,
        out_specs=VMEM,
        scratch_shapes=screen_scratch(count, width, height)
        + [pltpu.VMEM((4, 2) + columns[0].shape, BF16), kern, kern, part, part]
        + [pltpu.VMEM((2, states, states), F32), pltpu.SMEM((8,), F32)]
        + [pltpu.SMEM((20,), jnp.int32)]
        + [pltpu.SemaphoreType.DMA((count,))],
        compiler_params=pltpu.CompilerParams(vmem_limit_bytes=16 * 1024 * 1024),
        cost_estimate=pl.CostEstimate(
            flops=flops,
            bytes_accessed=8 * 1024 * 1024,
            transcendentals=count * 16 * width * height,
        ),
        interpret=INTERPRET,
        name="late_sum",
    )(nu, held, *early, *flat, *columns)


def screen_kernel(strength, pole, out, loaded, sems):
    copies = [
        pltpu.make_async_copy(strength, loaded.at[0], sems.at[0]),
        pltpu.make_async_copy(pole, loaded.at[1], sems.at[1]),
    ]
    for copy in copies:
        copy.start()
    for part, copy in enumerate(copies):
        copy.wait()
        out[part] = loaded[part].T


def front_screen(strength, pole):
    height, width = strength.shape
    return pl.pallas_call(
        screen_kernel,
        out_shape=jax.ShapeDtypeStruct((2, width, height), BF16),
        in_specs=[ANY] * 2,
        out_specs=VMEM,
        scratch_shapes=[pltpu.VMEM((2, height, width), BF16), pltpu.SemaphoreType.DMA((2,))],
        compiler_params=pltpu.CompilerParams(vmem_limit_bytes=SCREEN_VMEM),
        interpret=INTERPRET,
        name="front_screen",
    )(strength, pole)


def rows_kernel(energies, elements, own, part01, part10, part11, tall, sem):
    height, width = elements.shape[1], own.shape[1]
    copy = pltpu.make_async_copy(elements, tall.at[:, pl.ds(0, height), :], sem.at[0])
    copy.start()
    shape = (16, tall.shape[2])
    line = lax.broadcasted_iota(jnp.int32, shape, 0)
    for k in range(2):
        level = jnp.full(shape, energies[k], F32)
        high = level.astype(BF16).astype(F32)
        middle = (level - high).astype(BF16).astype(F32)
        low = level - high - middle
        value = jnp.where(line == 0, high, jnp.where(line == 1, middle, low))
        tall[k, pl.ds(height, 16), :] = value.astype(BF16)
    yl, yh = lax.axis_index("yl"), lax.axis_index("yh")
    copy.wait()
    for slot, out in enumerate((own, part01, part10, part11)):
        piece = (yl ^ (slot // 2)) * 2 + (yh ^ (slot % 2))
        out[...] = tall[:, pl.ds(pl.multiple_of(piece * width, width), width), :]


def front_rows(energies, elements, width):
    _, height, states = elements.shape
    piece = jax.ShapeDtypeStruct((2, width, states), BF16)
    return pl.pallas_call(
        rows_kernel,
        out_shape=(piece,) * 4 + (jax.ShapeDtypeStruct((2, height + 16, states), BF16),),
        in_specs=[SMEM, ANY],
        out_specs=(VMEM,) * 5,
        scratch_shapes=[pltpu.SemaphoreType.DMA((1,))],
        compiler_params=pltpu.CompilerParams(vmem_limit_bytes=ROWS_VMEM),
        interpret=INTERPRET,
        name="front_rows",
    )(energies, elements)


def turn_kernel(own, other0, other1, other2, out):
    width, states = own.shape[1:]
    for slot, ref in enumerate((own, other0, other1, other2)):
        out[slot] = ref[...].reshape(2 * width, states).T


def turn(own, others):
    width, states = own.shape[1:]
    vmem = pl.BlockSpec(memory_space=pltpu.VMEM)
    return pl.pallas_call(
        turn_kernel,
        out_shape=jax.ShapeDtypeStruct((4, states, 2 * width), BF16),
        in_specs=[vmem] * 4,
        out_specs=vmem,
        compiler_params=pltpu.CompilerParams(vmem_limit_bytes=4 * 1024 * 1024),
        interpret=INTERPRET,
        name="turn",
    )(own, *others)


def pair_kernel(first, second, out):
    out[0] = first[...]
    out[1] = second[...]


def pair_up(first, second):
    vmem = pl.BlockSpec(memory_space=pltpu.VMEM)
    return pl.pallas_call(
        pair_kernel,
        out_shape=jax.ShapeDtypeStruct((2,) + first.shape, first.dtype),
        in_specs=[vmem] * 2,
        out_specs=vmem,
        compiler_params=pltpu.CompilerParams(vmem_limit_bytes=4 * 1024 * 1024),
        interpret=INTERPRET,
    )(first, second)


def half_kernel(got, out):
    out[...] = jnp.sum(got[...].astype(F32), axis=0).T.astype(BF16)


def end_kernel(got, out):
    value = jnp.sum(got[...].astype(F32), axis=0)
    half = value.shape[1] // 2
    out[0] = value[:, :half]
    out[1] = value[:, half:]


def small(body, value, out_shape):
    vmem = pl.BlockSpec(memory_space=pltpu.VMEM)
    return pl.pallas_call(
        body,
        out_shape=out_shape,
        in_specs=[vmem],
        out_specs=vmem,
        compiler_params=pltpu.CompilerParams(vmem_limit_bytes=8 * 1024 * 1024),
        interpret=INTERPRET,
    )(value)


def on_device(elements, strength, pole_freq, energies, imag_freqs):
    band_count, row_count, states = elements.shape
    width = strength.shape[1]
    total_rows = row_count * 8
    scale = 1.0 / (total_rows * math.sqrt(band_count * 32))

    combos = ((0, 0), (0, 1), (1, 0), (1, 1))
    screen = front_screen(strength, pole_freq)
    own, *sent, tall = front_rows(energies, elements, width)

    held = move(screen, ("c", "yh"), lambda cc, hh: (hh, cc))

    others = [
        move(value, ("yl", "yh"), functools.partial(lambda a, b, l, h: (l ^ a, h ^ b), a, b))
        for (a, b), value in zip(combos[1:], sent)
    ]

    flip = lambda i: (i ^ 1,)
    both = pair_up(tall, move(tall, ("c",), flip))
    rows = [
        move(both, ("yl", "c", "yh"), functools.partial(lambda a, l, cc, h: (l ^ a, h, cc), a))
        for a in range(2)
    ]

    ahead = lambda i, cc: (i + 1 - 2 * cc, cc)
    moved = pair_up(held, move(held, ("c",), flip))
    pieces = [held]
    for _ in range(1, 4):
        moved = move(moved, ("z", "c"), ahead)
        pieces += [moved, move(moved, ("c",), flip)]
    pieces.append(move(moved[0], ("z", "c"), ahead))

    turned = turn(own, others)
    theirs = move(turned, ("c",), flip)
    behind = lambda cc, i: (cc, i - 1 + 2 * cc)
    near = move(pair_up(turned, theirs), ("c", "x"), behind)
    across = move(near[0], ("c", "x"), behind)
    columns = (turned, theirs, near, move(near, ("c",), flip), across, move(across, ("c",), flip))

    shape = (width, row_count, states)
    parts0, kept = early_sum(imag_freqs, pieces[:3], (None, 0, 1), rows, shape)
    (parts1,) = early_sum(imag_freqs, pieces[3:6], (0, 1, 0), [kept], shape)
    blocks = late_sum(
        scale, imag_freqs, kept, (parts0, parts1), pieces[6:], (1, None), columns, shape
    )
    got = lax.all_to_all(blocks, PW, 0, 0, tiled=True)
    part = small(half_kernel, got, jax.ShapeDtypeStruct((states, states // 4), BF16))
    part = lax.all_to_all(part.reshape(32, states // 32, states // 4), BAND, 0, 0, tiled=True)
    return small(end_kernel, part, jax.ShapeDtypeStruct((2, states // 32, states // 8), F32))


def solution(mesh):
    fine = Mesh(mesh.devices.reshape(8, 2, 2, 2, 4), ("z", "yl", "c", "yh", "x"))
    in_specs = (P(BAND, PW, None), P(PW, BAND), P(PW, BAND), P(BAND), P())
    out_specs = P(None, BAND, PW)
    return jax.shard_map(
        on_device, mesh=fine, in_specs=in_specs, out_specs=out_specs, check_vma=False
    )
```
